32 devices in a mesh: seq: 16 (over z, x, core), head: 2 (over y).
Axes of the slice: x: 2, y: 2, z: 4, core: 2. Of those that a mesh axis runs over, the one named last changes fastest.
Arguments:
- points: bfloat16 [16384, 512], P(('seq', 'head')), may hold values from -5000 to 5000
- norm_gain: float32 [512], replicated, may hold values from 0.1 to 1.9
- qkv_weight: bfloat16 [3, 512, 512], replicated, may hold values from -24 to 24
- out_weight: bfloat16 [512, 512], replicated, may hold values from -4 to 4
- neighbours: int32 [64, 8], replicated, may hold values from 0 to 63, as said below
Outputs:
- update: bfloat16 [16384, 512], P(('seq', 'head'))
The draws below stay inside these ranges and needn't reach their ends.
Inputs may be any that keep to these rules, and one draw needn't show every extreme that they name: `neighbours`: column 0 of row p is p. Columns 1 to 4 are distinct patches p + s with 0 < |s| <= 4. The last 3 columns name patches whose owner (patch // 4) is not the owner of p. Over all patches of one owner, the far columns name any one other owner at most 1 times, each time a different patch, and every owner reaches 1 with some other owner.
All inputs are finite; a program needn't handle non-finite values.
Results may differ from the reference program's by a relative error of at most 0.006.
The reference program's roundings to bfloat16 on the way (of `normed`, `weights` and `attended`) count: a program that leaves them out, or rounds other values in their place, can miss the bound.
Values may be sent and summed in bfloat16 or wider, within the bound.
No kernel may reach another device: no remote copies, remote signals or barrier semaphores. Data moves between devices by JAX's collectives and lax.ppermute only.
A program may use at most 64 MiB of HBM per device.

```python
import math
import jax
import jax.numpy as jnp
from jax import lax

D = 512
HEADS = 16
HEAD_DIM = 32
PATCH = 256
NEIGH = 8
NEAR = 4
FAR = 3
PATCH_DEV = 4
NPATCH = 64
TOKENS = 16384


def draw_points(key, part):
    keys_list = jax.random.split(jax.random.fold_in(key, 11), 3)
    base_normal = jax.random.truncated_normal(keys_list[0], -4.0, 4.0, (TOKENS, D), jnp.float32)
    position = jnp.arange(D, dtype=jnp.float32) / D
    jitter = jnp.exp(jax.random.uniform(keys_list[2], (D,), jnp.float32, -0.35, 0.35))
    row_scale = jnp.exp(jax.random.uniform(keys_list[1], (TOKENS, 1), jnp.float32, 0.0, math.log(10.0)))
    col_scale = jnp.exp(position * math.log(10.0)) * jitter
    return (base_normal * col_scale * row_scale).astype(jnp.bfloat16)


def draw_qkv_weight(key, part):
    base_normal = jax.random.truncated_normal(jax.random.fold_in(key, 17), -4.0, 4.0, (3, D, D), jnp.float32)
    scaled = base_normal * D ** (-0.5)
    return scaled.astype(jnp.bfloat16)


def draw_neighbours(key, part):
    keys_list = jax.random.split(jax.random.fold_in(key, 23), 4)
    shard_total = NPATCH // PATCH_DEV
    far_span = shard_total - 1
    patch_ids = jnp.arange(NPATCH, dtype=jnp.int32)
    ranking = jax.random.randint(keys_list[0], (NPATCH, PATCH_DEV), 0, 1 << 20) * PATCH_DEV + jnp.arange(PATCH_DEV, dtype=jnp.int32)[None, :]
    magnitudes = (jnp.argsort(ranking, axis=1)[:, :NEAR] + 1).astype(jnp.int32)
    signs = jax.random.randint(keys_list[1], (NPATCH, NEAR), 0, 2) * 2 - 1
    near_ids = patch_ids[:, None] + signs * magnitudes
    outside = (near_ids < 0) | (near_ids >= NPATCH)
    near_ids = jnp.where(outside, patch_ids[:, None] - signs * magnitudes, near_ids)
    owner_rank = jax.random.randint(keys_list[2], (shard_total, far_span), 0, 1 << 20) * far_span + jnp.arange(far_span, dtype=jnp.int32)[None, :]
    owner_order = jnp.argsort(owner_rank, axis=1).astype(jnp.int32)
    ref_ids = jnp.arange(PATCH_DEV * FAR, dtype=jnp.int32)
    shard_ids = jnp.arange(shard_total, dtype=jnp.int32)[:, None]
    owners = (shard_ids + 1 + owner_order[:, ref_ids % far_span]) % shard_total
    slot_ranks = ref_ids[None, :] // far_span
    offsets = jax.random.randint(keys_list[3], (shard_total, shard_total), 0, PATCH_DEV)
    local_ids = (jnp.take_along_axis(offsets, owners, axis=1) + slot_ranks) % PATCH_DEV
    far_ids = (owners * PATCH_DEV + local_ids).reshape(NPATCH, FAR)
    return jnp.concatenate([patch_ids[:, None], near_ids, far_ids], axis=1).astype(jnp.int32)


def normal_values(stream_key, extent, scale, limit, kind=jnp.bfloat16):
    values = jax.random.normal(stream_key, extent, jnp.float32) * scale
    return jnp.minimum(jnp.maximum(values, -limit), limit).astype(kind)


def setup_inputs(seed: int = 0) -> dict:
    keys = jax.random.split(jax.random.key(seed), 6)
    points = draw_points(jax.random.fold_in(keys[5], 71), 0)
    norm_gain = jnp.clip(1.0 + 0.18 * jax.random.normal(keys[1], (D,), jnp.float32), 0.1, 1.9)
    qkv_weight = draw_qkv_weight(jax.random.fold_in(keys[5], 71), 0)
    out_weight = normal_values(keys[3], (D, D), 0.7, 4.0)
    neighbours = draw_neighbours(jax.random.fold_in(keys[5], 71), 0)
    return dict(points=points, norm_gain=norm_gain, qkv_weight=qkv_weight, out_weight=out_weight, neighbours=neighbours)


EPS = 1e-06

def reference(points, norm_gain, qkv_weight, out_weight, neighbours):
    floats = points.astype(jnp.float32)
    mean_square = lax.optimization_barrier(jnp.sum(floats * floats, axis=1, keepdims=True)) / D
    normed = (floats * lax.rsqrt(mean_square + EPS) * norm_gain.astype(jnp.float32)).astype(jnp.bfloat16)
    query_proj = jnp.dot(normed, qkv_weight[0], preferred_element_type=jnp.float32).astype(jnp.bfloat16)
    key_proj = jnp.dot(normed, qkv_weight[1], preferred_element_type=jnp.float32).astype(jnp.bfloat16)
    value_proj = jnp.dot(normed, qkv_weight[2], preferred_element_type=jnp.float32).astype(jnp.bfloat16)
    query_blocks = query_proj.reshape(NPATCH, PATCH, HEADS, HEAD_DIM)
    key_blocks = key_proj.reshape(NPATCH, PATCH, HEADS, HEAD_DIM)
    value_blocks = value_proj.reshape(NPATCH, PATCH, HEADS, HEAD_DIM)

    def attend(patch_index):
        listed = neighbours[patch_index]
        query_rows = query_blocks[patch_index].astype(jnp.float32)
        listed_keys = key_blocks[listed].reshape(NEIGH * PATCH, HEADS, HEAD_DIM).astype(jnp.float32)
        listed_values = value_blocks[listed].reshape(NEIGH * PATCH, HEADS, HEAD_DIM).astype(jnp.float32)
        scores = jnp.einsum('qhd,khd->hqk', query_rows, listed_keys) * HEAD_DIM ** (-0.5)
        row_top = lax.optimization_barrier(jnp.max(scores, axis=2, keepdims=True))
        lifted = jnp.exp(scores - row_top)
        weights = (lifted / lax.optimization_barrier(jnp.sum(lifted, axis=2, keepdims=True))).astype(jnp.bfloat16)
        mixed_rows = jnp.einsum('hqk,khd->qhd', weights.astype(jnp.float32), listed_values)
        return mixed_rows.astype(jnp.bfloat16).reshape(PATCH, D)
    attended = lax.map(attend, jnp.arange(NPATCH, dtype=jnp.int32)).reshape(TOKENS, D)
    return jnp.dot(attended, out_weight, preferred_element_type=jnp.float32).astype(jnp.bfloat16)
```

```python
import functools
import math

import jax
import jax.numpy as jnp
from jax import lax
from jax.experimental import pallas as pl
from jax.experimental.pallas import tpu as pltpu
from jax.sharding import PartitionSpec as P

D = 512
HEAD_DIM = 32
PATCH = 256
NEIGH = 8
NEAR = 4
FAR = 3


EPS = 1e-06


def with_halo(cells, sides, width):
    for axis, dim in sides:
        count = lax.axis_size(axis)
        ends = count - 1
        head = lax.slice_in_dim(cells, 0, width, axis=dim)
        tail = lax.slice_in_dim(cells, cells.shape[dim] - width, cells.shape[dim], axis=dim)
        cells = jnp.concatenate(
            [
                lax.ppermute(tail, axis, [(i, (i + 1) % count) for i in range(ends)]),
                cells,
                lax.ppermute(head, axis, [((i + 1) % count, i) for i in range(ends)]),
            ],
            axis=dim,
        )
    return cells


def attend_patch(operands):
    query_rows, kv_rows = operands
    local_width = query_rows.shape[1]
    local_heads = local_width // HEAD_DIM
    query_rows = query_rows.reshape(PATCH, local_heads, HEAD_DIM)
    key_rows = kv_rows[:, :local_width].reshape(-1, local_heads, HEAD_DIM)
    values = kv_rows[:, local_width:].reshape(-1, local_heads, HEAD_DIM)
    scores = jnp.einsum(
        "qhd,khd->hqk", query_rows, key_rows, preferred_element_type=jnp.float32
    ) * HEAD_DIM ** (-0.5)
    row_top = jnp.max(scores, axis=2, keepdims=True)
    lifted = jnp.exp(scores - row_top)
    weights = (lifted / jnp.sum(lifted, axis=2, keepdims=True)).astype(jnp.bfloat16)
    mixed_rows = jnp.einsum("hqk,khd->qhd", weights, values, preferred_element_type=jnp.float32)
    return mixed_rows.astype(jnp.bfloat16).reshape(PATCH, local_width)


def gathered_body(points, norm_gain, qkv_weight, out_weight, neighbours):
    head_count = lax.axis_size("head")
    head_index = lax.axis_index("head")
    seq_count = lax.axis_size("seq")
    shard_index = lax.axis_index("seq")
    column_share = D // head_count
    floats = points.astype(jnp.float32)
    mean_square = jnp.sum(floats * floats, axis=1, keepdims=True) / D
    normed = (floats * lax.rsqrt(mean_square + EPS) * norm_gain).astype(jnp.bfloat16)
    grouped_weight = (
        qkv_weight.reshape(3, D, head_count, column_share)
        .transpose(1, 2, 0, 3)
        .reshape(D, head_count, 3 * column_share)
    )
    own_columns = lax.dynamic_index_in_dim(grouped_weight, head_index, 1, keepdims=False)
    projected = jnp.dot(
        lax.all_gather(normed, "head", axis=0, tiled=True),
        own_columns,
        preferred_element_type=jnp.float32,
    ).astype(jnp.bfloat16)
    row_count = projected.shape[0]
    per_shard = row_count // PATCH
    queries = projected[:, :column_share]
    kv_local = projected[:, column_share:].reshape(per_shard, PATCH, 2 * column_share)
    extended = with_halo(kv_local, (("seq", 0),), per_shard)
    own_lists = lax.dynamic_slice_in_dim(neighbours, shard_index * per_shard, per_shard, 0)
    near_index = own_lists[:, : 1 + NEAR] - (shard_index - 1) * per_shard
    near_rows = extended[near_index]
    ref_count = per_shard * FAR
    far_lists = neighbours[:, 1 + NEAR :].reshape(seq_count, ref_count)
    owners = far_lists // per_shard
    local_ids = far_lists % per_shard
    earlier = jnp.arange(ref_count)[None, :] < jnp.arange(ref_count)[:, None]
    same_owner = owners[:, :, None] == owners[:, None, :]
    slot_ranks = jnp.sum(same_owner & earlier[None], axis=2)
    slot_count = (FAR * per_shard + seq_count - 2) // (seq_count - 1)
    owned_refs = (owners == shard_index).astype(jnp.float32)
    slot_hot = (slot_ranks[:, :, None] == jnp.arange(slot_count)[None, None, :]).astype(jnp.float32)
    local_hot = (local_ids[:, :, None] == jnp.arange(per_shard)[None, None, :]).astype(jnp.float32)
    selector = jnp.einsum("rk,rkj,rkl->rjl", owned_refs, slot_hot, local_hot).astype(jnp.bfloat16)
    flat_kv = kv_local.reshape(per_shard, PATCH * 2 * column_share)
    outgoing = jnp.dot(
        selector.reshape(seq_count * slot_count, per_shard),
        flat_kv,
        preferred_element_type=jnp.float32,
    )
    outgoing = outgoing.astype(jnp.bfloat16).reshape(seq_count, slot_count, PATCH, 2 * column_share)
    incoming = lax.all_to_all(outgoing, "seq", split_axis=0, concat_axis=0, tiled=True)
    my_owners = lax.dynamic_index_in_dim(owners, shard_index, 0, keepdims=False)
    my_slots = lax.dynamic_index_in_dim(slot_ranks, shard_index, 0, keepdims=False)
    far_rows = incoming.reshape(seq_count * slot_count, PATCH, 2 * column_share)[
        my_owners * slot_count + my_slots
    ]
    far_rows = far_rows.reshape(per_shard, FAR, PATCH, 2 * column_share)
    gathered = jnp.concatenate([near_rows, far_rows], axis=1).reshape(
        per_shard, NEIGH * PATCH, 2 * column_share
    )
    attended = lax.map(
        attend_patch, (queries.reshape(per_shard, PATCH, column_share), gathered)
    ).reshape(row_count, column_share)
    owned_rows = lax.all_to_all(attended, "head", split_axis=0, concat_axis=1, tiled=True)
    update = jnp.dot(owned_rows, out_weight, preferred_element_type=jnp.float32).astype(
        jnp.bfloat16
    )
    return update


LANES = 128
SCALE = HEAD_DIM ** (-0.5) * math.log2(math.e)
ROW_BY_ROW = (((1,), (1,)), ((), ()))
VMEM = pl.BlockSpec(memory_space=pltpu.VMEM)
SMEM = pl.BlockSpec(memory_space=pltpu.SMEM)


def kernel_params():
    return pltpu.CompilerParams(vmem_limit_bytes=60 * 2**20)


def dot_bf16(rows, weight):
    return jnp.dot(rows, weight, preferred_element_type=jnp.float32).astype(jnp.bfloat16)


def attend_lanes(query, keys, values, tops_before=None):
    head_of_lane = lax.broadcasted_iota(jnp.int32, (1, LANES), 1) // HEAD_DIM
    sums = None
    tops = jnp.zeros((query.shape[0], LANES), jnp.float32)
    for head in range(LANES // HEAD_DIM):
        mine = head_of_lane == head
        masked = jnp.where(mine, query, jnp.zeros_like(query))
        scores = [
            lax.dot_general(masked, k, ROW_BY_ROW, preferred_element_type=jnp.float32)
            for k in keys
        ]
        top = functools.reduce(jnp.maximum, scores)
        top = jnp.max(top, axis=1, keepdims=True)
        if tops_before is not None:
            top = jnp.maximum(top, tops_before[:, head * HEAD_DIM : head * HEAD_DIM + 1])
        for block, v in zip(scores, values):
            lifted = jnp.exp2((block - top) * SCALE).astype(jnp.bfloat16)
            mine_rows = jnp.broadcast_to(mine, v.shape)
            wide = jnp.concatenate(
                [jnp.where(mine, v, jnp.zeros_like(v)), mine_rows.astype(v.dtype)], axis=1
            )
            part = jnp.dot(lifted, wide, preferred_element_type=jnp.float32)
            sums = part if sums is None else sums + part
        tops = jnp.where(mine, top, tops)
    return sums[:, :LANES], sums[:, LANES:], tops


def block_of(index, size):
    return pl.ds(pl.multiple_of(index * size, size), size)


def near_kernel(pieces, own, slots, *refs):
    count = 1 + max(piece[0] for piece in pieces)
    arrays, (weight, mixed, total, tops, queries, keys, values) = refs[:count], refs[count:]
    queries[...] = dot_bf16(arrays[own][...], weight[0])
    for array, source, size, target in pieces:
        rows = arrays[array][source : source + size, :]
        keys[target : target + size, :] = dot_bf16(rows, weight[1])
        values[target : target + size, :] = dot_bf16(rows, weight[2])
    groups = queries.shape[1] // LANES
    listed = slots.shape[1]

    def step(i, carry):
        patch, lanes = i // groups, block_of(i % groups, LANES)
        rows = block_of(patch, PATCH)
        spans = [block_of(slots[patch, n], PATCH) for n in range(listed)]
        mixed[rows, lanes], total[rows, lanes], tops[rows, lanes] = attend_lanes(
            queries[rows, lanes],
            [keys[span, lanes] for span in spans],
            [values[span, lanes] for span in spans],
        )
        return carry

    lax.fori_loop(0, queries.shape[0] // PATCH * groups, step, 0)


def near_part(slots, arrays, pieces, own, weight):
    rows, width = arrays[own].shape
    window = max(target + size for _, _, size, target in pieces)
    wide = jax.ShapeDtypeStruct((rows, width), jnp.float32)
    flops = 2 * (rows + 2 * window) * width * width + 4 * rows * slots.shape[1] * PATCH * width * 4
    return pl.pallas_call(
        functools.partial(near_kernel, pieces, own),
        in_specs=[SMEM] + [VMEM] * (len(arrays) + 1),
        out_specs=[VMEM] * 4,
        out_shape=[wide, wide, wide, jax.ShapeDtypeStruct((rows, width), jnp.bfloat16)],
        scratch_shapes=[pltpu.VMEM((window, width), jnp.bfloat16)] * 2,
        compiler_params=kernel_params(),
        cost_estimate=pl.CostEstimate(flops=flops, bytes_accessed=8 * 2**20, transcendentals=0),
        name="near_part",
    )(slots, *arrays, weight)


def far_kernel(slots, halves, others, weight, out_weight, queries, mixed, total, tops, update, rows_in, keys, values, attended):
    patches, listed = slots.shape
    half = halves.shape[1]
    for n in range(patches * listed):
        rows_in[n * PATCH : n * PATCH + half, :] = halves[slots[n // listed, n % listed]]
        rows_in[n * PATCH + half : (n + 1) * PATCH, :] = others[n]
    for n in range(patches * listed):
        span = slice(n * PATCH, (n + 1) * PATCH)
        keys[span, :] = dot_bf16(rows_in[span, :], weight[1])
        values[span, :] = dot_bf16(rows_in[span, :], weight[2])
    groups = queries.shape[1] // LANES

    def step(i, carry):
        patch, lanes = i // groups, block_of(i % groups, LANES)
        rows = block_of(patch, PATCH)
        spans = [block_of(patch * listed + n, PATCH) for n in range(listed)]
        before = tops[rows, lanes]
        mixed_now, total_now, tops_now = attend_lanes(
            queries[rows, lanes],
            [keys[span, lanes] for span in spans],
            [values[span, lanes] for span in spans],
            before,
        )
        keep = jnp.exp2((before - tops_now) * SCALE)
        mixed_now += mixed[rows, lanes] * keep
        total_now += total[rows, lanes] * keep
        attended[rows, lanes] = (mixed_now / total_now).astype(jnp.bfloat16)
        return carry

    lax.fori_loop(0, patches * groups, step, 0)
    update[...] = dot_bf16(attended[...], out_weight[...])


def far_part(slots, halves, others, weight, out_weight, state):
    rows, width = state[0].shape
    window = slots.shape[0] * slots.shape[1] * PATCH
    mixed, total, tops, queries = state
    flops = 2 * (rows + 2 * window) * width * width + 4 * rows * slots.shape[1] * PATCH * width * 4
    return pl.pallas_call(
        far_kernel,
        in_specs=[SMEM] + [VMEM] * 8,
        out_specs=VMEM,
        out_shape=jax.ShapeDtypeStruct((rows, width), jnp.bfloat16),
        scratch_shapes=[pltpu.VMEM((window, width), jnp.bfloat16)] * 3
        + [pltpu.VMEM((rows, width), jnp.bfloat16)],
        compiler_params=kernel_params(),
        cost_estimate=pl.CostEstimate(flops=flops, bytes_accessed=8 * 2**20, transcendentals=0),
        name="far_part",
    )(slots, halves, others, weight, out_weight, queries, mixed, total, tops)


def spread_kernel(picks, place, own, got, out):
    target = pl.program_id(0)
    patch, from_own = picks[0, target], picks[1, target]
    half = out.shape[1]

    @pl.when(from_own == 1)
    def _():
        start = pl.multiple_of(patch * PATCH + place[0] * half, half)
        out[0] = own[pl.ds(start, half), :]

    @pl.when(from_own == 0)
    def _():
        out[0] = got[patch]


def spread(picks, place, own, got):
    count = picks.shape[1]
    half, width = got.shape[1:]
    return pl.pallas_call(
        spread_kernel,
        grid=(count,),
        in_specs=[SMEM, SMEM, VMEM, VMEM],
        out_specs=pl.BlockSpec((1, half, width), lambda i: (i, 0, 0)),
        out_shape=jax.ShapeDtypeStruct((count, half, width), jnp.bfloat16),
        compiler_params=kernel_params(),
        name="spread",
    )(picks, place, own, got)


def shifted(rows, axis, by):
    count = lax.axis_size(axis)
    pairs = [(i, i + by) for i in range(count) if 0 <= i + by < count]
    return lax.ppermute(rows, axis, pairs)


def swapped(rows):
    return lax.ppermute(rows, "head", [(0, 1), (1, 0)])


def paired_body(points, norm_gain, qkv_weight, out_weight, neighbours):
    head_index = lax.axis_index("head")
    seq_count = lax.axis_size("seq")
    shard_index = lax.axis_index("seq")
    rows, width = points.shape
    patches = rows // PATCH
    per_shard = 2 * patches
    half = PATCH // 2
    floats = points.astype(jnp.float32)
    mean_square = jnp.sum(floats * floats, axis=1, keepdims=True) / D
    normed = (floats * lax.rsqrt(mean_square + EPS) * norm_gain).astype(jnp.bfloat16)

    halves = normed.reshape(patches, 2, half, width)
    got_mine = swapped(lax.dynamic_index_in_dim(halves, 1 - head_index, 1, keepdims=False))
    earlier = shifted(normed, "seq", 1)
    later = shifted(normed, "seq", -1)
    got_rest = swapped(lax.dynamic_index_in_dim(halves, head_index, 1, keepdims=False))
    relayed = swapped(jnp.where(head_index == 0, later, earlier))

    far_lists = neighbours[:, 1 + NEAR :].reshape(seq_count, per_shard * FAR)
    owners, locals_ = far_lists // per_shard, far_lists % per_shard
    wanted = jnp.sum(jnp.where(owners == shard_index, locals_, 0), axis=1)
    picks = jnp.stack([wanted % patches, (wanted // patches == head_index).astype(jnp.int32)])
    outgoing = spread(picks, head_index.reshape(1), normed, got_mine)
    incoming = lax.all_to_all(outgoing, "seq", split_axis=0, concat_axis=0, tiled=True)

    my_owners = lax.dynamic_index_in_dim(owners, shard_index, 0, keepdims=False).reshape(2, -1)
    own_slots = lax.dynamic_index_in_dim(my_owners, head_index, 0, keepdims=False)
    their_slots = lax.dynamic_index_in_dim(my_owners, 1 - head_index, 0, keepdims=False)
    others = swapped(incoming[their_slots])

    device = shard_index * 2 + head_index
    near_lists = lax.dynamic_slice_in_dim(neighbours, device * patches, patches, 0)[:, : 1 + NEAR]
    places = near_lists - (device - 2) * patches
    block, inside = places // patches, places % patches
    block = jnp.where((head_index == 0) & (block % 2 == 1), 4 - block, block)
    arrays = [
        earlier,
        got_mine.reshape(rows // 2, width),
        got_rest.reshape(rows // 2, width),
        normed,
        relayed,
        later,
    ]
    pieces = [(0, 0, rows, 0), (3, 0, rows, 2 * rows), (4, 0, rows, 3 * rows), (5, 0, rows, 4 * rows)]
    for n in range(patches):
        pieces.append((1, n * half, half, rows + n * PATCH))
        pieces.append((2, n * half, half, rows + n * PATCH + half))
    state = near_part(block * patches + inside, arrays, pieces, 3, qkv_weight)
    return far_part(
        own_slots.reshape(patches, FAR), incoming, others, qkv_weight, out_weight, state
    )


def solution(mesh):
    body = paired_body if mesh.shape["head"] == 2 else gathered_body
    placed = (P(("seq", "head"), None), P(), P(), P(), P())
    return jax.shard_map(
        body, mesh=mesh, in_specs=placed, out_specs=P(("seq", "head"), None), check_vma=False
    )
```
